32 devices in a mesh: seq: 16 (over z, y, x), tp: 2 (over core).
Axes of the slice: x: 2, y: 2, z: 4, core: 2. Of those that a mesh axis runs over, the one named last changes fastest.
Arguments:
- ssm_inputs: bfloat16 [4096, 4096], P('seq', 'tp'), may hold values from -6 to 6
- write_proj: bfloat16 [4096, 128], P('seq'), may hold values from -6 to 6
- read_proj: bfloat16 [4096, 128], P('seq'), may hold values from -0.5 to 0.5
- log_decay: float32 [4096, 64], P('seq', 'tp'), may hold values from -1 to 0, as said below
- skip_gain: float32 [64], P('tp'), may hold values from 0.5 to 1.5
- norm_gain: float32 [4096], replicated, may hold values from 0.1 to 1.9
- gate_weight: bfloat16 [7168, 4096], P('tp', 'seq'), may hold values from -0.09375 to 0.09375
- up_weight: bfloat16 [7168, 4096], P('tp', 'seq'), may hold values from -0.09375 to 0.09375
- down_weight: bfloat16 [7168, 4096], P('tp', 'seq'), may hold values from -0.09375 to 0.09375
Outputs:
- ssd_out: bfloat16 [4096, 4096], P('seq', 'tp')
- mixed: bfloat16 [4096, 4096], P('seq', 'tp')
The draws below stay inside these ranges and needn't reach their ends.
Inputs may be any that keep to these rules, and one draw needn't show every extreme that they name: `log_decay`: every entry is negative.
All inputs are finite; a program needn't handle non-finite values.
Results may differ from the reference program's by a relative error of at most 0.015.
Values may be sent and summed in bfloat16 or wider, within the bound.
A program may use at most 192 MiB of HBM per device.

```python
import jax
import jax.numpy as jnp
from jax import lax

D = 4096
HEADS = 64
HEAD_DIM = 64
STATE = 128
FF = 7168
BLOCK = 128
TOK_DEV = 256
SPAN_EXTENT = 4096
FF_BLOCK = 3584


def draw_log_decay(key, part):
    keys = jax.random.split(jax.random.fold_in(key, 17), 7)
    slow_heads = jax.random.bernoulli(keys[0], 0.5, (HEADS,))
    slow_rate = jnp.exp(jax.random.uniform(keys[1], (HEADS,), jnp.float32, jnp.log(0.05), jnp.log(0.5))) / SPAN_EXTENT
    fast_rate = jnp.exp(jax.random.uniform(keys[2], (HEADS,), jnp.float32, jnp.log(1.0 / 50.0), jnp.log(1.0 / 25.0)))
    forgetting_speed = jnp.where(slow_heads, slow_rate, fast_rate)
    element_factor = jax.random.uniform(keys[3], (SPAN_EXTENT, HEADS), jnp.float32, 0.5, 1.5)
    shard_factor = jnp.exp(jax.random.uniform(keys[4], (SPAN_EXTENT // TOK_DEV, HEADS), jnp.float32, -0.5, 0.5))
    shard_factor = jnp.repeat(shard_factor, TOK_DEV, axis=0)
    layout_indices = jax.random.randint(keys[5], (3,), 0, SPAN_EXTENT)
    segment_bundles = jnp.any(jnp.arange(SPAN_EXTENT)[:, None] == layout_indices[None, :], axis=1)
    objective_scores = jnp.log(jax.random.uniform(keys[6], (SPAN_EXTENT, HEADS), jnp.float32, 0.6, 0.8))
    ultimate_output_array = -forgetting_speed[None, :] * element_factor * shard_factor + jnp.where(segment_bundles[:, None], objective_scores, 0.0)
    return ultimate_output_array.astype(jnp.float32)


def strengthened(result, key, source, target, blocks, factor):
    owner, partner = [(jnp.arange(result.shape[dim]) // (result.shape[dim] // blocks)).reshape([-1 if axis == dim else 1 for axis in range(result.ndim)]) for dim in (source, target)]
    chosen = jax.random.permutation(key, blocks)[partner]
    strong = (owner == chosen) | (owner == (partner + blocks // 2) % blocks)
    return jnp.where(strong, factor * result, result)


def shard_levels(own_key, extent, cuts, low, largest):
    factor_of, own = 1.0, jax.random.fold_in(own_key, 6)
    for axis_at, parts in cuts:
        draws = jnp.exp(jax.random.uniform(jax.random.fold_in(own, axis_at), (parts,), jnp.float32, low / len(cuts), largest / len(cuts)))
        factor_of = factor_of * jnp.repeat(draws, extent[axis_at] // parts).reshape([-1 if axis == axis_at else 1 for axis in range(len(extent))])
    return factor_of


def noise(stream_key, extent, deviation, bound, cuts=(), dtype=jnp.bfloat16):
    result = deviation * jax.random.normal(stream_key, extent, jnp.float32)
    if cuts:
        result = result * shard_levels(stream_key, extent, cuts, -0.22, 0.18)
    return jnp.clip(result, -bound, bound).astype(dtype)


def noise_with(own_key, extent, scale, bound, cuts, heavy, dtype=jnp.bfloat16):
    array = scale * jax.random.normal(own_key, extent, jnp.float32)
    if cuts:
        array = array * shard_levels(own_key, extent, cuts, -0.22, 0.18)
    return jnp.clip(strengthened(array, jax.random.fold_in(own_key, 3), *heavy), -bound, bound).astype(dtype)


def setup_inputs(seed: int = 0) -> dict:
    key_list = jax.random.split(jax.random.key(seed), 10)
    ssm_inputs = noise(key_list[0], (SPAN_EXTENT, D), 1.0, 6.0, ((0, 16), (1, 2)))
    write_proj = noise(key_list[1], (SPAN_EXTENT, STATE), 1.0, 6.0, ((0, 16),))
    read_proj = noise(key_list[2], (SPAN_EXTENT, STATE), STATE ** -0.5, 0.5, ((0, 16),))
    log_decay = draw_log_decay(jax.random.fold_in(key_list[9], 71), 0)
    skip_gain = jnp.clip(0.5 + 1.0 * jax.random.uniform(key_list[4], (HEADS,), jnp.float32) ** shard_levels(key_list[4], (HEADS,), ((0, 2),), -0.2, 0.2), 0.5, 1.5)
    norm_gain = jnp.clip(1.0 + 0.18 * jax.random.normal(key_list[5], (D,), jnp.float32), 0.1, 1.9)
    gate_weight = noise(key_list[6], (FF, D), D ** -0.5, 0.09375, ((0, 2), (1, 16)))
    up_weight = noise(key_list[7], (FF, D), D ** -0.5, 0.09375, ((0, 2), (1, 16)))
    down_weight = noise_with(key_list[8], (FF, D), FF ** -0.5, 0.09375, ((0, 2), (1, 16)), (0, 1, 16, 2.0))
    return {"ssm_inputs": ssm_inputs, "write_proj": write_proj, "read_proj": read_proj, "log_decay": log_decay, "skip_gain": skip_gain, "norm_gain": norm_gain, "gate_weight": gate_weight, "up_weight": up_weight, "down_weight": down_weight}


HIGHEST = lax.Precision.HIGHEST

def block_step(carried_state, pieces):
    feature_rows, write_rows, read_rows, decay_rows = pieces
    scaled = feature_rows * jnp.sqrt(-jnp.expm1(2.0 * decay_rows))[:, :, None]
    running = jnp.cumsum(decay_rows, axis=0)
    span_len = decay_rows.shape[0]
    causal = jnp.arange(span_len)[:, None] >= jnp.arange(span_len)[None, :]
    spread_log = running[:, None, :] - running[None, :, :]
    weights = jnp.exp(jnp.where(causal[:, :, None], spread_log, -jnp.inf))
    scores = jnp.dot(read_rows, write_rows.T, precision=HIGHEST)
    within = jnp.einsum('ijh,jhp->ihp', scores[:, :, None] * weights, scaled, precision=HIGHEST)
    arriving = jnp.exp(running)[:, :, None] * jnp.einsum('hpn,in->ihp', carried_state, read_rows, precision=HIGHEST)
    to_end = jnp.exp(running[-1][None, :] - running)
    written = jnp.einsum('jhp,jn->hpn', scaled * to_end[:, :, None], write_rows, precision=HIGHEST)
    next_state = jnp.exp(running[-1])[:, None, None] * carried_state + written
    return (next_state, within + arriving)

def reference(ssm_inputs, write_proj, read_proj, log_decay, skip_gain, norm_gain, gate_weight, up_weight, down_weight):
    block_count = SPAN_EXTENT // BLOCK
    features = ssm_inputs.astype(jnp.float32).reshape(SPAN_EXTENT, HEADS, HEAD_DIM)
    writes = write_proj.astype(jnp.float32)
    reads = read_proj.astype(jnp.float32)
    start_state = jnp.zeros((HEADS, HEAD_DIM, STATE), jnp.float32)
    pieces = (features.reshape(block_count, BLOCK, HEADS, HEAD_DIM), writes.reshape(block_count, BLOCK, STATE), reads.reshape(block_count, BLOCK, STATE), log_decay.reshape(block_count, BLOCK, HEADS))
    final_state, outputs = lax.scan(block_step, start_state, pieces)
    combined = outputs.reshape(SPAN_EXTENT, HEADS, HEAD_DIM) + skip_gain[None, :, None] * features
    ssd_out = combined.reshape(SPAN_EXTENT, D).astype(jnp.bfloat16)
    rows_f = ssd_out.astype(jnp.float32)
    mean_sq = lax.optimization_barrier(jnp.mean(rows_f * rows_f, axis=1, keepdims=True))
    normed = (rows_f * lax.rsqrt(mean_sq + 1e-05) * norm_gain[None, :]).astype(jnp.bfloat16)
    tp_count = FF // FF_BLOCK
    stacked = (gate_weight.reshape(tp_count, FF_BLOCK, D), up_weight.reshape(tp_count, FF_BLOCK, D), down_weight.reshape(tp_count, FF_BLOCK, D))

    def add_block(mlp_sum, weights_block):
        gate_rows, up_rows, down_rows = weights_block
        gate_act = lax.dot_general(normed, gate_rows, (((1,), (1,)), ((), ())), preferred_element_type=jnp.float32)
        up_act = lax.dot_general(normed, up_rows, (((1,), (1,)), ((), ())), preferred_element_type=jnp.float32)
        hidden = (jax.nn.silu(gate_act) * up_act).astype(jnp.bfloat16)
        partial_value = jnp.dot(hidden, down_rows, preferred_element_type=jnp.float32).astype(jnp.bfloat16)
        partial_value = lax.optimization_barrier(partial_value)
        return (mlp_sum + partial_value.astype(jnp.float32), None)
    mlp_sum, unused = lax.scan(add_block, jnp.zeros((SPAN_EXTENT, D), jnp.float32), stacked)
    mixed = (rows_f + mlp_sum).astype(jnp.bfloat16)
    return (ssd_out, mixed)
```

```python
import functools

import jax
import jax.numpy as jnp
from jax import lax
from jax.experimental import pallas as pl
from jax.experimental.pallas import tpu as pltpu
from jax.sharding import PartitionSpec as P

MINOR = 4
BF = jnp.bfloat16
F32 = jnp.float32


def flip(b, m):
    if m == 0:
        return b
    if m == 1:
        return b + 1 - 2 * (b % 2)
    if m == 2:
        return (b + 2) % 4
    return 3 - b


def along_major(x, step, n):
    major = n // MINOR
    route = [
        (a * MINOR + b, ((a + step) % major) * MINOR + b)
        for a in range(major)
        for b in range(MINOR)
    ]
    return lax.ppermute(x, "seq", route)


def along_minor(x, m, n):
    route = [(i, (i // MINOR) * MINOR + flip(i % MINOR, m)) for i in range(n)]
    return lax.ppermute(x, "seq", route)


def nt(x, w):
    return lax.dot_general(x, w, (((1,), (1,)), ((), ())), preferred_element_type=F32)


def piece_ref(refs, k, m):
    group, at = refs[5 * (k // 2) : 5 * (k // 2) + 5], k % 2
    if m < 3:
        return group[m].at[at]
    return group[3 + at].at[0]


def gate_up_kernel(major, depth, *args):
    count = 5 * major // 2
    x_ref, w_refs = args[0], args[1 : 1 + count]
    h_ref, wbuf, acc, sem = args[1 + count :]
    rows = x_ref.shape[0]
    tile = min(rows, 256)
    me = lax.axis_index("seq")
    a, b = me // MINOR, me % MINOR

    def fetch(k):
        return [
            pltpu.make_async_copy(
                piece_ref(w_refs, k, m).at[pl.ds(0, 2)], wbuf.at[k % 2, m], sem.at[k % 2, m]
            )
            for m in range(MINOR)
        ]

    for c in fetch(0):
        c.start()
    for k in range(major):
        if k + 1 < major:
            for c in fetch(k + 1):
                c.start()
        for c in fetch(k):
            c.wait()
        src = (a + major - k) % major
        cols = [
            pl.ds(pl.multiple_of((src * MINOR + flip(b, m)) * depth, depth), depth)
            for m in range(MINOR)
        ]

        @pl.loop(0, rows // tile)
        def _(i):
            at = pl.ds(pl.multiple_of(i * tile, tile), tile)
            sums = [None, None]
            for m in range(MINOR):
                x = x_ref[at, cols[m]]
                for q in range(2):
                    d = nt(x, wbuf[k % 2, m, q])
                    sums[q] = d if sums[q] is None else sums[q] + d
            if k > 0:
                sums = [acc[q, at, :] + sums[q] for q in range(2)]
            if k + 1 < major:
                for q in range(2):
                    acc[q, at, :] = sums[q]
            else:
                g, u = sums
                h_ref[at, :] = (g / (1.0 + jnp.exp(-g)) * u).astype(BF)


def down_kernel(major, depth, *args):
    count = 5 * major // 2
    h_ref, w_refs = args[0], args[1 : 1 + count]
    o_ref, wbuf, obuf, sem, osem = args[1 + count :]
    rows = h_ref.shape[0]
    tile = min(rows, 256)
    me = lax.axis_index("seq")
    a, b = me // MINOR, me % MINOR
    steps = [(k, m) for k in range(major) for m in range(MINOR)]

    def fetch(j):
        k, m = steps[j]
        return pltpu.make_async_copy(piece_ref(w_refs, k, m).at[2], wbuf.at[j % 2], sem.at[j % 2])

    def put(j):
        k, m = steps[j]
        src = (a + major - k) % major
        col = pl.multiple_of((src * MINOR + flip(b, m)) * depth, depth)
        return pltpu.make_async_copy(obuf.at[j % 2], o_ref.at[:, pl.ds(col, depth)], osem.at[j % 2])

    fetch(0).start()
    for j in range(len(steps)):
        if j + 1 < len(steps):
            fetch(j + 1).start()
        fetch(j).wait()
        if j >= 2:
            put(j - 2).wait()

        @pl.loop(0, rows // tile)
        def _(i):
            at = pl.ds(pl.multiple_of(i * tile, tile), tile)
            obuf[j % 2, at, :] = jnp.dot(
                h_ref[at, :], wbuf[j % 2], preferred_element_type=F32
            ).astype(BF)

        put(j).start()
    put(len(steps) - 2).wait()
    put(len(steps) - 1).wait()


ANY = pl.BlockSpec(memory_space=pl.ANY)
INV = pl.BlockSpec(memory_space=pltpu.VMEM)


def feed_forward(normed, pieces, major, depth):
    rows, width = normed.shape
    units = pieces[0].shape[2]
    hidden = pl.pallas_call(
        functools.partial(gate_up_kernel, major, depth),
        out_shape=jax.ShapeDtypeStruct((rows, units), BF),
        in_specs=[INV] + [ANY] * len(pieces),
        out_specs=INV,
        scratch_shapes=[
            pltpu.VMEM((2, MINOR, 2, units, depth), BF),
            pltpu.VMEM((2, rows, units), F32),
            pltpu.SemaphoreType.DMA((2, MINOR)),
        ],
        compiler_params=pltpu.CompilerParams(vmem_limit_bytes=56 << 20),
        cost_estimate=pl.CostEstimate(
            flops=4 * rows * units * width, bytes_accessed=4 * units * width, transcendentals=0
        ),
    )(normed, *pieces)
    return pl.pallas_call(
        functools.partial(down_kernel, major, depth),
        out_shape=jax.ShapeDtypeStruct((rows, width), BF),
        in_specs=[INV] + [ANY] * len(pieces),
        out_specs=ANY,
        scratch_shapes=[
            pltpu.VMEM((2, units, depth), BF),
            pltpu.VMEM((2, rows, depth), BF),
            pltpu.SemaphoreType.DMA((2,)),
            pltpu.SemaphoreType.DMA((2,)),
        ],
        compiler_params=pltpu.CompilerParams(vmem_limit_bytes=40 << 20),
        cost_estimate=pl.CostEstimate(
            flops=2 * rows * units * width, bytes_accessed=4 * units * width, transcendentals=0
        ),
    )(hidden, *pieces)


def on_device(
    ssm_inputs,
    write_proj,
    read_proj,
    log_decay,
    skip_gain,
    norm_gain,
    gate_weight,
    up_weight,
    down_weight,
):
    n = lax.axis_size("seq")
    tp = lax.axis_size("tp")
    major = n // MINOR
    me = lax.axis_index("seq")
    a = me // MINOR
    toks, feats = ssm_inputs.shape
    heads = log_decay.shape[1]
    hdim = feats // heads
    states = write_proj.shape[1]
    units, depth = gate_weight.shape
    part = units // major

    stacked = jnp.stack([w.reshape(major, part, depth) for w in (gate_weight, up_weight, down_weight)])

    def chunk(k):
        return lax.dynamic_index_in_dim(stacked, (a + k) % major, axis=1, keepdims=False)

    got = [chunk(0)] + [along_major(chunk(k), k, n) for k in range(1, major)]
    pieces = []
    for g in range(0, major, 2):
        own = jnp.stack(got[g : g + 2])
        over_x = along_minor(own, 1, n)
        over_y = along_minor(own, 2, n)
        first = along_minor(over_x[:1], 2, n)
        second = along_minor(over_y[1:], 1, n)
        pieces += [own, over_x, over_y, first, second]

    x = ssm_inputs.astype(F32).reshape(toks, heads, hdim)
    scaled = x * jnp.sqrt(-jnp.expm1(2.0 * log_decay))[:, :, None]
    running = jnp.cumsum(log_decay, axis=0)
    total = running[-1]
    to_end = jnp.exp(total[None, :] - running)
    local_final = lax.dot_general(
        (scaled * to_end[:, :, None]).astype(BF).reshape(toks, feats),
        write_proj,
        (((0,), (0,)), ((), ())),
        preferred_element_type=F32,
    )
    rows = feats // n
    row_total = jnp.repeat(total, hdim).reshape(n, rows)
    finals = lax.all_to_all(
        local_final.astype(BF).reshape(n, rows, states), "seq", 0, 0, tiled=True
    ).astype(F32)
    decays = jnp.exp(lax.all_to_all(row_total, "seq", 0, 0, tiled=True))
    state = jnp.zeros((rows, states), F32)
    before = []
    for j in range(n):
        before.append(state.astype(BF))
        if j + 1 < n:
            state = decays[j][:, None] * state + finals[j]
    incoming = lax.all_to_all(jnp.stack(before), "seq", 0, 0, tiled=True).reshape(feats, states)

    scores = nt(read_proj, write_proj)
    r = running.T
    causal = jnp.arange(toks)[:, None] >= jnp.arange(toks)[None, :]
    weights = jnp.exp(jnp.where(causal[None], r[:, :, None] - r[:, None, :], -jnp.inf))
    mixing = (scores[None] * weights).astype(BF)
    within = jnp.einsum(
        "hij,hjp->hip", mixing, scaled.astype(BF).transpose(1, 0, 2), preferred_element_type=F32
    ).transpose(1, 0, 2)
    arriving = nt(read_proj, incoming).reshape(toks, heads, hdim)
    combined = within + jnp.exp(running)[:, :, None] * arriving + skip_gain[None, :, None] * x
    ssd_out = combined.reshape(toks, feats).astype(BF)

    rows_f = ssd_out.astype(F32)
    square_sum = lax.psum(jnp.sum(rows_f * rows_f, axis=1, keepdims=True), "tp")
    gain = lax.dynamic_slice_in_dim(norm_gain, lax.axis_index("tp") * feats, feats)
    normed = (rows_f * lax.rsqrt(square_sum / (feats * tp) + 1e-05) * gain[None, :]).astype(BF)

    group = jnp.concatenate([normed] + [along_major(normed, k, n) for k in range(1, major)], axis=0)
    group = lax.all_gather(group, "tp", axis=1, tiled=True)
    partial = feed_forward(group, pieces, major, depth)
    own = lax.psum_scatter(partial, "tp", scatter_dimension=1, tiled=True)
    own = own.reshape(major, toks, feats)
    mlp = own[0].astype(F32)
    for k in range(1, major):
        mlp = mlp + along_major(own[k], major - k, n).astype(F32)
    mixed = (rows_f + mlp).astype(BF)
    return (ssd_out, mixed)


def solution(mesh):
    placed = (
        P("seq", "tp"),
        P("seq", None),
        P("seq", None),
        P("seq", "tp"),
        P("tp"),
        P(),
        P("tp", "seq"),
        P("tp", "seq"),
        P("tp", "seq"),
    )
    return jax.shard_map(
        on_device,
        mesh=mesh,
        in_specs=placed,
        out_specs=(P("seq", "tp"), P("seq", "tp")),
        check_vma=False,
    )
```

```python
import functools

import jax
import jax.numpy as jnp
from jax import lax
from jax.experimental import pallas as pl
from jax.experimental.pallas import tpu as pltpu
from jax.sharding import PartitionSpec as P

MINOR = 4
BF = jnp.bfloat16
F32 = jnp.float32


def flip(b, m):
    if m == 0:
        return b
    if m == 1:
        return b + 1 - 2 * (b % 2)
    if m == 2:
        return (b + 2) % 4
    return 3 - b


def along_major(x, step, n):
    major = n // MINOR
    route = [
        (a * MINOR + b, ((a + step) % major) * MINOR + b)
        for a in range(major)
        for b in range(MINOR)
    ]
    return lax.ppermute(x, "seq", route)


def along_minor(x, m, n):
    route = [(i, (i // MINOR) * MINOR + flip(i % MINOR, m)) for i in range(n)]
    return lax.ppermute(x, "seq", route)


def nt(x, w):
    return lax.dot_general(x, w, (((1,), (1,)), ((), ())), preferred_element_type=F32)


def piece_ref(refs, k, m):
    group, at = refs[5 * (k // 2) : 5 * (k // 2) + 5], k % 2
    if m < 3:
        return group[m].at[at]
    return group[3 + at].at[0]


def gate_up_kernel(major, depth, *args):
    count = 5 * major // 2
    x_ref, w_refs = args[0], args[1 : 1 + count]
    h_ref, wbuf, acc, sem = args[1 + count :]
    _, rows, width = x_ref.shape
    tile = min(rows, 256)
    me = lax.axis_index("seq")
    a, b = me // MINOR, me % MINOR

    def fetch(k):
        return [
            pltpu.make_async_copy(
                piece_ref(w_refs, k, m).at[pl.ds(0, 2)], wbuf.at[k % 2, m], sem.at[k % 2, m]
            )
            for m in range(MINOR)
        ]

    for c in fetch(0):
        c.start()
    for k in range(major):
        if k + 1 < major:
            for c in fetch(k + 1):
                c.start()
        for c in fetch(k):
            c.wait()
        src = (a + major - k) % major
        starts = [(src * MINOR + flip(b, m)) * depth for m in range(MINOR)]

        @pl.loop(0, rows // tile)
        def _(i):
            at = pl.ds(pl.multiple_of(i * tile, tile), tile)
            sums = [None, None]
            for m in range(MINOR):
                x = x_ref[starts[m] // width, at, pl.ds(pl.multiple_of(starts[m] % width, depth), depth)]
                for q in range(2):
                    d = nt(x, wbuf[k % 2, m, q])
                    sums[q] = d if sums[q] is None else sums[q] + d
            if k > 0:
                sums = [acc[q, at, :] + sums[q] for q in range(2)]
            if k + 1 < major:
                for q in range(2):
                    acc[q, at, :] = sums[q]
            else:
                g, u = sums
                h_ref[at, :] = (g / (1.0 + jnp.exp(-g)) * u).astype(BF)


def down_kernel(major, depth, *args):
    count = 5 * major // 2
    h_ref, w_refs = args[0], args[1 : 1 + count]
    o_ref, wbuf, obuf, sem, osem = args[1 + count :]
    rows = h_ref.shape[0]
    width = o_ref.shape[2]
    tile = min(rows, 256)
    me = lax.axis_index("seq")
    a, b = me // MINOR, me % MINOR
    steps = [(k, m) for k in range(major) for m in range(MINOR)]

    def fetch(j):
        k, m = steps[j]
        return pltpu.make_async_copy(piece_ref(w_refs, k, m).at[2], wbuf.at[j % 2], sem.at[j % 2])

    def put(j):
        k, m = steps[j]
        src = (a + major - k) % major
        start = (src * MINOR + flip(b, m)) * depth
        col = pl.ds(pl.multiple_of(start % width, depth), depth)
        return pltpu.make_async_copy(
            obuf.at[j % 2], o_ref.at[start // width, :, col], osem.at[j % 2]
        )

    fetch(0).start()
    for j in range(len(steps)):
        if j + 1 < len(steps):
            fetch(j + 1).start()
        fetch(j).wait()
        if j >= 2:
            put(j - 2).wait()

        @pl.loop(0, rows // tile)
        def _(i):
            at = pl.ds(pl.multiple_of(i * tile, tile), tile)
            obuf[j % 2, at, :] = jnp.dot(
                h_ref[at, :], wbuf[j % 2], preferred_element_type=F32
            ).astype(BF)

        put(j).start()
    put(len(steps) - 2).wait()
    put(len(steps) - 1).wait()


def prefix_kernel(finals_ref, decay_ref, o_ref):
    n, rows, states = o_ref.shape
    state = jnp.zeros((rows, states), F32)
    for j in range(n):
        o_ref[j] = state.astype(BF)
        state = decay_ref[j] * state + finals_ref[j, pl.ds(0, rows), :].astype(F32)


ANY = pl.BlockSpec(memory_space=pl.ANY)
INV = pl.BlockSpec(memory_space=pltpu.VMEM)


def feed_forward(normed, pieces, major, depth):
    shares, rows, share = normed.shape
    width = shares * share
    units = pieces[0].shape[2]
    hidden = pl.pallas_call(
        functools.partial(gate_up_kernel, major, depth),
        out_shape=jax.ShapeDtypeStruct((rows, units), BF),
        in_specs=[INV] + [ANY] * len(pieces),
        out_specs=INV,
        scratch_shapes=[
            pltpu.VMEM((2, MINOR, 2, units, depth), BF),
            pltpu.VMEM((2, rows, units), F32),
            pltpu.SemaphoreType.DMA((2, MINOR)),
        ],
        compiler_params=pltpu.CompilerParams(vmem_limit_bytes=56 << 20),
        cost_estimate=pl.CostEstimate(
            flops=4 * rows * units * width, bytes_accessed=4 * units * width, transcendentals=0
        ),
    )(normed, *pieces)
    return pl.pallas_call(
        functools.partial(down_kernel, major, depth),
        out_shape=jax.ShapeDtypeStruct(normed.shape, BF),
        in_specs=[INV] + [ANY] * len(pieces),
        out_specs=ANY,
        scratch_shapes=[
            pltpu.VMEM((2, units, depth), BF),
            pltpu.VMEM((2, rows, depth), BF),
            pltpu.SemaphoreType.DMA((2,)),
            pltpu.SemaphoreType.DMA((2,)),
        ],
        compiler_params=pltpu.CompilerParams(vmem_limit_bytes=40 << 20),
        cost_estimate=pl.CostEstimate(
            flops=2 * rows * units * width, bytes_accessed=4 * units * width, transcendentals=0
        ),
    )(hidden, *pieces)


def share_features(x):
    if lax.axis_size("tp") != 2:
        return lax.all_gather(x, "tp", axis=1, tiled=True)[None]
    other = lax.ppermute(x, "tp", [(0, 1), (1, 0)])
    first = lax.axis_index("tp") == 0
    return jnp.stack([jnp.where(first, x, other), jnp.where(first, other, x)])


def own_features(partial):
    if lax.axis_size("tp") != 2:
        return lax.psum_scatter(partial[0], "tp", scatter_dimension=1, tiled=True)
    t = lax.axis_index("tp")
    give = lax.dynamic_index_in_dim(partial, 1 - t, axis=0, keepdims=False)
    keep = lax.dynamic_index_in_dim(partial, t, axis=0, keepdims=False)
    come = lax.ppermute(give, "tp", [(0, 1), (1, 0)])
    return (keep.astype(F32) + come.astype(F32)).astype(BF)


def on_device(
    ssm_inputs,
    write_proj,
    read_proj,
    log_decay,
    skip_gain,
    norm_gain,
    gate_weight,
    up_weight,
    down_weight,
):
    n = lax.axis_size("seq")
    tp = lax.axis_size("tp")
    major = n // MINOR
    me = lax.axis_index("seq")
    a = me // MINOR
    toks, feats = ssm_inputs.shape
    heads = log_decay.shape[1]
    hdim = feats // heads
    states = write_proj.shape[1]
    units, depth = gate_weight.shape
    part = units // major

    stacked = jnp.stack([w.reshape(major, part, depth) for w in (gate_weight, up_weight, down_weight)])

    def chunk(k):
        return lax.dynamic_index_in_dim(stacked, (a + k) % major, axis=1, keepdims=False)

    got = [chunk(0)] + [along_major(chunk(k), k, n) for k in range(1, major)]

    x = ssm_inputs.astype(F32).reshape(toks, heads, hdim)
    scaled = x * jnp.sqrt(-jnp.expm1(2.0 * log_decay))[:, :, None]
    running = jnp.cumsum(log_decay, axis=0)
    total = running[-1]
    to_end = jnp.exp(total[None, :] - running)
    local_final = lax.dot_general(
        (scaled * to_end[:, :, None]).astype(BF).reshape(toks, feats),
        write_proj,
        (((0,), (0,)), ((), ())),
        preferred_element_type=F32,
    )
    rows = feats // n
    decay = jnp.repeat(jnp.exp(total), hdim).reshape(n, 1, rows)
    high = decay.astype(BF)
    low = (decay - high.astype(F32)).astype(BF)
    extra = jnp.concatenate([high, low, jnp.zeros((n, 14, rows), BF)], axis=1)
    extra = jnp.pad(extra, ((0, 0), (0, 0), (0, states - rows)))
    payload = jnp.concatenate([local_final.astype(BF).reshape(n, rows, states), extra], axis=1)
    finals = lax.all_to_all(payload, "seq", 0, 0, tiled=True)
    decays = finals[:, rows, :rows].astype(F32) + finals[:, rows + 1, :rows].astype(F32)
    before = pl.pallas_call(
        prefix_kernel,
        out_shape=jax.ShapeDtypeStruct((n, rows, states), BF),
        in_specs=[INV, INV],
        out_specs=INV,
    )(finals, decays[:, :, None])
    before, got[1] = lax.optimization_barrier((before, got[1]))
    incoming = lax.all_to_all(before, "seq", 0, 0, tiled=True).reshape(feats, states)
    incoming, *got[2:] = lax.optimization_barrier((incoming, *got[2:]))

    def first_hops(g):
        own = jnp.stack(got[g : g + 2])
        return [own, along_minor(own, 1, n), along_minor(own, 2, n)]

    def second_hops(hops):
        return [along_minor(hops[1][:1], 2, n), along_minor(hops[2][1:], 1, n)]

    scores = nt(read_proj, write_proj)
    r = running.T
    causal = jnp.arange(toks)[:, None] >= jnp.arange(toks)[None, :]
    weights = jnp.exp(jnp.where(causal[None], r[:, :, None] - r[:, None, :], -jnp.inf))
    mixing = (scores[None] * weights).astype(BF)
    within = jnp.einsum(
        "hij,hjp->hip", mixing, scaled.astype(BF).transpose(1, 0, 2), preferred_element_type=F32
    ).transpose(1, 0, 2)
    arriving = nt(read_proj, incoming).reshape(toks, heads, hdim)
    combined = within + jnp.exp(running)[:, :, None] * arriving + skip_gain[None, :, None] * x
    ssd_out = combined.reshape(toks, feats).astype(BF)

    rows_f = ssd_out.astype(F32)
    square_sum = lax.psum(jnp.sum(rows_f * rows_f, axis=1, keepdims=True), "tp")
    gain = lax.dynamic_slice_in_dim(norm_gain, lax.axis_index("tp") * feats, feats)
    normed = (rows_f * lax.rsqrt(square_sum / (feats * tp) + 1e-05) * gain[None, :]).astype(BF)

    groups = [first_hops(g) for g in range(0, major, 2)]
    normed, groups[0] = lax.optimization_barrier((normed, groups[0]))
    tokens = [normed] + [along_major(normed, k, n) for k in range(1, major)]
    cut = major // 2 + 1
    pieces = groups[0] + second_hops(groups[0])
    tokens[1:cut], groups[1:], pieces = lax.optimization_barrier(
        (tokens[1:cut], groups[1:], pieces)
    )
    pieces = pieces + sum([g + second_hops(g) for g in groups[1:]], [])

    order = list(range(1, major)) + [0]
    backs = []
    for half in (order[: major // 2], order[major // 2 :]):
        some = jnp.concatenate([tokens[k] for k in half], axis=0)
        partial = feed_forward(share_features(some), pieces, major, depth)
        if backs:
            partial, backs = lax.optimization_barrier((partial, backs))
        own = own_features(partial).reshape(len(half), toks, feats)
        backs += [along_major(own[i], major - k, n) if k else own[i] for i, k in enumerate(half)]
    mlp = sum(back.astype(F32) for back in backs)
    mixed = (rows_f + mlp).astype(BF)
    return (ssd_out, mixed)


def solution(mesh):
    placed = (
        P("seq", "tp"),
        P("seq", None),
        P("seq", None),
        P("seq", "tp"),
        P("tp"),
        P(),
        P("tp", "seq"),
        P("tp", "seq"),
        P("tp", "seq"),
    )
    return jax.shard_map(
        on_device,
        mesh=mesh,
        in_specs=placed,
        out_specs=(P("seq", "tp"), P("seq", "tp")),
        check_vma=False,
    )
```

```python
import functools

import jax
import jax.numpy as jnp
from jax import lax
from jax.experimental import pallas as pl
from jax.experimental.pallas import tpu as pltpu
from jax.sharding import PartitionSpec as P

MINOR = 4
PIECES = 13
BF = jnp.bfloat16
F32 = jnp.float32


def flip(b, m):
    if m == 0:
        return b
    if m == 1:
        return b + 1 - 2 * (b % 2)
    if m == 2:
        return (b + 2) % 4
    return 3 - b


def along_major(x, step, n):
    major = n // MINOR
    route = [
        (a * MINOR + b, ((a + step) % major) * MINOR + b)
        for a in range(major)
        for b in range(MINOR)
    ]
    return lax.ppermute(x, "seq", route)


def along_minor(x, m, n):
    route = [(i, (i // MINOR) * MINOR + flip(i % MINOR, m)) for i in range(n)]
    return lax.ppermute(x, "seq", route)


def nt(x, w):
    return lax.dot_general(x, w, (((1,), (1,)), ((), ())), preferred_element_type=F32)


def near_steps(major):
    return [k for k in range(1, major) if k != major // 2]


def piece_ref(refs, major, k, m, q):
    own0, x0, y0, d0, e0, near, near_x, near_y, by_1, by_2, far, d_far, e_far = refs
    half = (major - 2) // 2
    if k == 0:
        return (own0, x0, y0)[m].at[q] if m < 3 else (d0.at[q] if q < 2 else e0.at[0])
    if k == major // 2:
        if m == 0:
            return far.at[q]
        if m < 3:
            return (by_1, by_2)[m - 1].at[3 * half + q]
        return d_far.at[q] if q < 2 else e_far.at[0]
    i = near_steps(major).index(k)
    if m < 3:
        return (near, near_x, near_y)[m].at[3 * i + q]
    return by_2.at[3 * i + q] if i < half else by_1.at[3 * (i - half) + q]


def gate_up_kernel(major, depth, *args):
    count = PIECES
    x_ref, w_refs = args[0], args[1 : 1 + count]
    h_ref, wbuf, acc, sem = args[1 + count :]
    _, rows, width = x_ref.shape
    tile = min(rows, 256)
    me = lax.axis_index("seq")
    a, b = me // MINOR, me % MINOR

    def fetch(k):
        return [
            pltpu.make_async_copy(
                piece_ref(w_refs, major, k, m, q), wbuf.at[k % 2, m, q], sem.at[k % 2, m, q]
            )
            for m in range(MINOR)
            for q in range(2)
        ]

    for c in fetch(0):
        c.start()
    for k in range(major):
        if k + 1 < major:
            for c in fetch(k + 1):
                c.start()
        for c in fetch(k):
            c.wait()
        src = (a + major - k) % major
        starts = [(src * MINOR + flip(b, m)) * depth for m in range(MINOR)]

        @pl.loop(0, rows // tile)
        def _(i):
            at = pl.ds(pl.multiple_of(i * tile, tile), tile)
            sums = [None, None]
            for m in range(MINOR):
                x = x_ref[starts[m] // width, at, pl.ds(pl.multiple_of(starts[m] % width, depth), depth)]
                for q in range(2):
                    d = nt(x, wbuf[k % 2, m, q])
                    sums[q] = d if sums[q] is None else sums[q] + d
            if k > 0:
                sums = [acc[q, at, :] + sums[q] for q in range(2)]
            if k + 1 < major:
                for q in range(2):
                    acc[q, at, :] = sums[q]
            else:
                g, u = sums
                h_ref[at, :] = (g / (1.0 + jnp.exp(-g)) * u).astype(BF)


def down_kernel(major, depth, *args):
    count = PIECES
    h_ref, w_refs = args[0], args[1 : 1 + count]
    o_ref, wbuf, obuf, sem, osem = args[1 + count :]
    rows = h_ref.shape[0]
    width = o_ref.shape[2]
    tile = min(rows, 256)
    me = lax.axis_index("seq")
    a, b = me // MINOR, me % MINOR
    steps = [(k, m) for k in range(major) for m in range(MINOR)]

    def fetch(j):
        k, m = steps[j]
        return pltpu.make_async_copy(piece_ref(w_refs, major, k, m, 2), wbuf.at[j % 2], sem.at[j % 2])

    def put(j):
        k, m = steps[j]
        src = (a + major - k) % major
        start = (src * MINOR + flip(b, m)) * depth
        col = pl.ds(pl.multiple_of(start % width, depth), depth)
        return pltpu.make_async_copy(
            obuf.at[j % 2], o_ref.at[start // width, :, col], osem.at[j % 2]
        )

    fetch(0).start()
    for j in range(len(steps)):
        if j + 1 < len(steps):
            fetch(j + 1).start()
        fetch(j).wait()
        if j >= 2:
            put(j - 2).wait()

        @pl.loop(0, rows // tile)
        def _(i):
            at = pl.ds(pl.multiple_of(i * tile, tile), tile)
            obuf[j % 2, at, :] = jnp.dot(
                h_ref[at, :], wbuf[j % 2], preferred_element_type=F32
            ).astype(BF)

        put(j).start()
    put(len(steps) - 2).wait()
    put(len(steps) - 1).wait()


def prefix_kernel(finals_ref, decay_ref, o_ref):
    n, rows, states = o_ref.shape
    state = jnp.zeros((rows, states), F32)
    for j in range(n):
        o_ref[j] = state.astype(BF)
        state = decay_ref[j] * state + finals_ref[j, pl.ds(0, rows), :].astype(F32)


ANY = pl.BlockSpec(memory_space=pl.ANY)
INV = pl.BlockSpec(memory_space=pltpu.VMEM)


def feed_forward(normed, pieces, major, depth):
    shares, rows, share = normed.shape
    width = shares * share
    units = pieces[0].shape[1]
    hidden = pl.pallas_call(
        functools.partial(gate_up_kernel, major, depth),
        out_shape=jax.ShapeDtypeStruct((rows, units), BF),
        in_specs=[INV] + [ANY] * len(pieces),
        out_specs=INV,
        scratch_shapes=[
            pltpu.VMEM((2, MINOR, 2, units, depth), BF),
            pltpu.VMEM((2, rows, units), F32),
            pltpu.SemaphoreType.DMA((2, MINOR, 2)),
        ],
        compiler_params=pltpu.CompilerParams(vmem_limit_bytes=56 << 20),
        cost_estimate=pl.CostEstimate(
            flops=4 * rows * units * width, bytes_accessed=4 * units * width, transcendentals=0
        ),
    )(normed, *pieces)
    return pl.pallas_call(
        functools.partial(down_kernel, major, depth),
        out_shape=jax.ShapeDtypeStruct(normed.shape, BF),
        in_specs=[INV] + [ANY] * len(pieces),
        out_specs=ANY,
        scratch_shapes=[
            pltpu.VMEM((2, units, depth), BF),
            pltpu.VMEM((2, rows, depth), BF),
            pltpu.SemaphoreType.DMA((2,)),
            pltpu.SemaphoreType.DMA((2,)),
        ],
        compiler_params=pltpu.CompilerParams(vmem_limit_bytes=40 << 20),
        cost_estimate=pl.CostEstimate(
            flops=2 * rows * units * width, bytes_accessed=4 * units * width, transcendentals=0
        ),
    )(hidden, *pieces)


def share_features(x):
    if lax.axis_size("tp") != 2:
        return lax.all_gather(x, "tp", axis=1, tiled=True)[None]
    other = lax.ppermute(x, "tp", [(0, 1), (1, 0)])
    first = lax.axis_index("tp") == 0
    return jnp.stack([jnp.where(first, x, other), jnp.where(first, other, x)])


def own_features(partial):
    if lax.axis_size("tp") != 2:
        return lax.psum_scatter(partial[0], "tp", scatter_dimension=1, tiled=True)
    t = lax.axis_index("tp")
    give = lax.dynamic_index_in_dim(partial, 1 - t, axis=0, keepdims=False)
    keep = lax.dynamic_index_in_dim(partial, t, axis=0, keepdims=False)
    come = lax.ppermute(give, "tp", [(0, 1), (1, 0)])
    return (keep.astype(F32) + come.astype(F32)).astype(BF)


def return_tokens(partial, steps, major, n):
    own = own_features(partial)
    own = own.reshape(len(steps), own.shape[0] // len(steps), own.shape[1])
    return [along_major(own[i], major - k, n) if k else own[i] for i, k in enumerate(steps)]


def on_device(
    ssm_inputs,
    write_proj,
    read_proj,
    log_decay,
    skip_gain,
    norm_gain,
    gate_weight,
    up_weight,
    down_weight,
):
    n = lax.axis_size("seq")
    tp = lax.axis_size("tp")
    major = n // MINOR
    me = lax.axis_index("seq")
    a = me // MINOR
    toks, feats = ssm_inputs.shape
    heads = log_decay.shape[1]
    hdim = feats // heads
    states = write_proj.shape[1]
    units, depth = gate_weight.shape
    part = units // major

    stacked = jnp.stack([w.reshape(major, part, depth) for w in (gate_weight, up_weight, down_weight)])

    def chunk(k):
        return lax.dynamic_index_in_dim(stacked, (a + k) % major, axis=1, keepdims=False)

    far = major // 2
    near = near_steps(major)
    half = 3 * len(near) // 2
    got = [along_major(chunk(k), k, n) for k in near]
    own = chunk(0)
    pieces = [own, along_minor(own, 1, n), along_minor(own, 2, n)]

    x = ssm_inputs.astype(F32).reshape(toks, heads, hdim)
    scaled = x * jnp.sqrt(-jnp.expm1(2.0 * log_decay))[:, :, None]
    running = jnp.cumsum(log_decay, axis=0)
    total = running[-1]
    to_end = jnp.exp(total[None, :] - running)
    local_final = lax.dot_general(
        (scaled * to_end[:, :, None]).astype(BF).reshape(toks, feats),
        write_proj,
        (((0,), (0,)), ((), ())),
        preferred_element_type=F32,
    )
    rows = feats // n
    decay = jnp.repeat(jnp.exp(total), hdim).reshape(n, 1, rows)
    high = decay.astype(BF)
    low = (decay - high.astype(F32)).astype(BF)
    extra = jnp.concatenate([high, low, jnp.zeros((n, 14, rows), BF)], axis=1)
    extra = jnp.pad(extra, ((0, 0), (0, 0), (0, states - rows)))
    payload = jnp.concatenate([local_final.astype(BF).reshape(n, rows, states), extra], axis=1)
    finals = lax.all_to_all(payload, "seq", 0, 0, tiled=True)
    decays = finals[:, rows, :rows].astype(F32) + finals[:, rows + 1, :rows].astype(F32)
    before = pl.pallas_call(
        prefix_kernel,
        out_shape=jax.ShapeDtypeStruct((n, rows, states), BF),
        in_specs=[INV, INV],
        out_specs=INV,
    )(finals, decays[:, :, None])
    before, pieces = lax.optimization_barrier((before, pieces))
    incoming = lax.all_to_all(before, "seq", 0, 0, tiled=True).reshape(feats, states)
    pieces += [along_minor(pieces[1][:2], 2, n), along_minor(pieces[2][2:], 1, n)]
    far_chunk = chunk(far)
    incoming, far_chunk, got, pieces = lax.optimization_barrier((incoming, far_chunk, got, pieces))
    far_own = along_major(far_chunk, far, n)
    group = jnp.concatenate(got)
    pieces += [group, along_minor(group, 1, n), along_minor(group, 2, n)]

    scores = nt(read_proj, write_proj)
    r = running.T
    causal = jnp.arange(toks)[:, None] >= jnp.arange(toks)[None, :]
    weights = jnp.exp(jnp.where(causal[None], r[:, :, None] - r[:, None, :], -jnp.inf))
    mixing = (scores[None] * weights).astype(BF)
    within = jnp.einsum(
        "hij,hjp->hip", mixing, scaled.astype(BF).transpose(1, 0, 2), preferred_element_type=F32
    ).transpose(1, 0, 2)
    arriving = nt(read_proj, incoming).reshape(toks, heads, hdim)
    combined = within + jnp.exp(running)[:, :, None] * arriving + skip_gain[None, :, None] * x
    ssd_out = combined.reshape(toks, feats).astype(BF)

    rows_f = ssd_out.astype(F32)
    square_sum = lax.psum(jnp.sum(rows_f * rows_f, axis=1, keepdims=True), "tp")
    gain = lax.dynamic_slice_in_dim(norm_gain, lax.axis_index("tp") * feats, feats)
    normed = (rows_f * lax.rsqrt(square_sum / (feats * tp) + 1e-05) * gain[None, :]).astype(BF)

    normed, far_own, pieces = lax.optimization_barrier((normed, far_own, pieces))
    tokens = [normed] + [along_major(normed, k, n) for k in range(1, major)]
    by_1 = along_minor(jnp.concatenate([pieces[7][half:], far_own]), 1, n)
    by_2 = along_minor(jnp.concatenate([pieces[6][:half], far_own]), 2, n)
    cut = major // 2 + 1
    tokens[1:cut], by_1, by_2 = lax.optimization_barrier((tokens[1:cut], by_1, by_2))
    last = [along_minor(by_1[half : half + 2], 2, n), along_minor(by_2[half + 2 :], 1, n)]
    pieces += [by_1, by_2, far_own] + last

    order = list(range(1, major)) + [0]
    backs, partial = [], None
    for half in (order[:far], order[far:]):
        some = [tokens[k] for k in half]
        if partial is not None:
            some, partial = lax.optimization_barrier((some, partial))
            backs = return_tokens(partial, order[:far], major, n)
        after = feed_forward(share_features(jnp.concatenate(some)), pieces, major, depth)
        if partial is not None:
            after, backs = lax.optimization_barrier((after, backs))
        partial = after
    backs = backs + return_tokens(partial, order[far:], major, n)
    mlp = sum(back.astype(F32) for back in backs)
    mixed = (rows_f + mlp).astype(BF)
    return (ssd_out, mixed)


def solution(mesh):
    placed = (
        P("seq", "tp"),
        P("seq", None),
        P("seq", None),
        P("seq", "tp"),
        P("tp"),
        P(),
        P("tp", "seq"),
        P("tp", "seq"),
        P("tp", "seq"),
    )
    return jax.shard_map(
        on_device,
        mesh=mesh,
        in_specs=placed,
        out_specs=(P("seq", "tp"), P("seq", "tp")),
        check_vma=False,
    )
```
